512 devices in a mesh: group: 32 (over x, y, core), tp: 16 (over z).
Axes of the slice: x: 4, y: 4, z: 16, core: 2. Of those that a mesh axis runs over, the one named last changes fastest.
Arguments:
- tokens: bfloat16 [24576, 8192], P('group', 'tp'), may hold values from -6 to 6
- w_query: bfloat16 [8192, 4096], P(None, 'tp'), may hold values from -0.0625 to 0.0625
- adapter_down: bfloat16 [384, 16, 8192], P('group', None, 'tp'), may hold values from -0.0625 to 0.0625
- adapter_up: bfloat16 [384, 16, 4096], P('group', None, 'tp'), may hold values from -1.5 to 1.5
- adapter_id: int32 [24576], P('group'), may hold values from 0 to 383, as said below
Outputs:
- query: bfloat16 [24576, 4096], P('group', 'tp')
The draws below stay inside these ranges and needn't reach their ends.
Inputs may be any that keep to these rules, and one draw needn't show every extreme that they name: `adapter_id`: adapter a is owned by group a // 12. Among the 768 requests of one group (an aligned block), at most 48 use adapters of any one owner; in every draw one owner receives exactly 48 from every group.
All inputs are finite; a program needn't handle non-finite values.
Results may differ from the reference program's by a relative error of at most 0.014.
Values may be sent and summed in bfloat16 or wider, within the bound.
No kernel may reach another device: no remote copies, remote signals or barrier semaphores. Data moves between devices by JAX's collectives and lax.ppermute only.
A program may use at most 128 MiB of HBM per device.

```python
import math
import jax
import jax.numpy as jnp
from jax import lax

D = 8192
RANK = 16
ADP_DEV = 12
REQ_DEV = 768
HO = 4096
ADAPTERS = 384
REQS = 24576
CAP = 48


def draw_adapter_id(key, part):
    group_count = ADAPTERS // ADP_DEV
    slot_count = group_count * CAP
    hot_owner = jax.random.randint(jax.random.fold_in(key, 7), (), 0, group_count)

    def one_group(group_key):
        key_order, key_shuffle, key_first, key_second = jax.random.split(group_key, 4)
        owner_of = jnp.arange(slot_count, dtype=jnp.int32) // CAP
        match_scores = jax.random.permutation(key_order, slot_count).astype(jnp.int32)
        match_scores = jnp.where(owner_of == hot_owner, match_scores - slot_count, match_scores)
        order = jnp.argsort(match_scores, stable=True)
        owners = owner_of[order[:REQ_DEV]]
        shuffle = jax.random.permutation(key_shuffle, REQ_DEV)
        owners = owners[shuffle]
        first = jax.random.randint(key_first, (REQ_DEV,), 0, ADP_DEV)
        second = jax.random.randint(key_second, (REQ_DEV,), 0, ADP_DEV)
        local = jnp.minimum(first, second)
        return (owners * ADP_DEV + local).astype(jnp.int32)
    serving_group_keys = jax.vmap(lambda number: jax.random.fold_in(key, number))(jnp.arange(group_count))
    return jax.vmap(one_group)(serving_group_keys).reshape(REQS).astype(jnp.int32)


def block_levels(own_key, shape, pieces, smallest, high):
    level, own = 1.0, jax.random.fold_in(own_key, 6)
    for dim, shards_of in pieces:
        heights = jnp.exp(jax.random.uniform(jax.random.fold_in(own, dim), (shards_of,), jnp.float32, smallest / len(pieces), high / len(pieces)))
        level = level * jnp.repeat(heights, shape[dim] // shards_of).reshape([-1 if axis == dim else 1 for axis in range(len(shape))])
    return level


def normal_values(rng, dims, spread, reach, shards=(), kind=jnp.bfloat16):
    entries = spread * jax.random.normal(rng, dims, jnp.float32)
    if shards:
        entries = entries * block_levels(rng, dims, shards, -0.22, 0.18)
    return jnp.clip(entries, -reach, reach).astype(kind)


def setup_inputs(seed: int = 0) -> dict:
    arg_keys = jax.random.split(jax.random.key(seed), 6)
    tokens = normal_values(arg_keys[0], (REQS, D), 1.0, 6.0, ((0, 32), (1, 16)))
    w_query = normal_values(arg_keys[1], (D, HO), D ** -0.5, 0.0625, ((1, 16),))
    adapter_down = normal_values(arg_keys[2], (ADAPTERS, RANK, D), D ** -0.5, 0.0625, ((0, 32), (2, 16)))
    adapter_up = normal_values(arg_keys[3], (ADAPTERS, RANK, HO), RANK ** -0.5, 1.5, ((0, 32), (2, 16)))
    adapter_id = draw_adapter_id(jax.random.fold_in(arg_keys[5], 71), 0)
    return {"tokens": tokens, "w_query": w_query, "adapter_down": adapter_down, "adapter_up": adapter_up, "adapter_id": adapter_id}


def reference(tokens, w_query, adapter_down, adapter_up, adapter_id):
    base = jnp.dot(tokens, w_query, preferred_element_type=jnp.float32)
    block_rows = math.gcd(REQS, 256)
    blocks = REQS // block_rows
    token_block_rows = tokens.reshape(blocks, block_rows, D)
    id_blocks = adapter_id.reshape(blocks, block_rows)

    def one_block(pair):
        token_rows, id_rows = pair
        picked_down = jnp.take(adapter_down, id_rows, axis=0).astype(jnp.float32)
        down = jnp.einsum("nd,nrd->nr", token_rows.astype(jnp.float32), picked_down)
        scaled_delta = (2.0 * down).astype(jnp.bfloat16)
        picked_up = jnp.take(adapter_up, id_rows, axis=0).astype(jnp.float32)
        delta = jnp.einsum("nr,nrh->nh", scaled_delta.astype(jnp.float32), picked_up)
        return delta.astype(jnp.bfloat16)

    delta = lax.map(one_block, (token_block_rows, id_blocks)).reshape(REQS, HO)
    return (base + delta.astype(jnp.float32)).astype(jnp.bfloat16)
```

```python
import jax
import jax.numpy as jnp
from jax import lax
from jax.sharding import PartitionSpec as P

adapter_scale_factor = 2.0
owner_slots = 48
F32, BF16 = jnp.float32, jnp.bfloat16


def slot_of_request(adapter_id, groups, per_group):
    n = adapter_id.shape[0]
    owner = adapter_id // per_group
    to_owner = owner[:, None] == lax.broadcasted_iota(jnp.int32, (n, groups), 1)
    before = lax.broadcasted_iota(jnp.int32, (n, n), 0) > lax.broadcasted_iota(jnp.int32, (n, n), 1)
    count = jnp.dot(before.astype(BF16), to_owner.astype(BF16), preferred_element_type=F32)
    rank = jnp.sum(jnp.where(to_owner, count, 0.0), axis=1).astype(jnp.int32)
    return owner * owner_slots + rank


def lora(tokens, adapter_down, adapter_up, adapter_id, groups, tp):
    n, d = tokens.shape
    per_group, rank, _ = adapter_down.shape
    ho = adapter_up.shape[2]
    slots = groups * owner_slots
    slot = slot_of_request(adapter_id, groups, per_group)
    place = (lax.broadcasted_iota(jnp.int32, (slots, n), 0) == slot[None, :]).astype(BF16)
    out_rows = jnp.dot(place, tokens, preferred_element_type=F32).astype(BF16)
    local = (adapter_id % per_group).astype(BF16)
    out_ids = jnp.dot(place, local[:, None], preferred_element_type=F32).astype(BF16)
    out_ids = out_ids.reshape(groups, 1, owner_slots)
    out_ids = jnp.pad(out_ids, ((0, 0), (0, 7), (0, d - owner_slots)))
    sent = jnp.concatenate([out_rows.reshape(groups, owner_slots, d), out_ids], axis=1)
    here = lax.all_to_all(sent, "group", 0, 0, tiled=True)
    rows = here[:, :owner_slots].reshape(slots, d)
    ids = here[:, owner_slots, :owner_slots].astype(jnp.int32).reshape(1, 1, slots)
    mine = lax.broadcasted_iota(jnp.int32, (per_group, 1, slots), 0) == ids
    part = lax.dot_general(
        adapter_down.reshape(per_group * rank, d), rows, (((1,), (1,)), ((), ())), preferred_element_type=F32
    ).reshape(per_group, rank, slots)
    part = jnp.sum(jnp.where(mine, part, 0.0), axis=0)
    share = rank // tp
    part = lax.all_to_all(part.reshape(tp, share, slots), "tp", 0, 0, tiled=True)
    scaled = (adapter_scale_factor * jnp.sum(part, axis=0)).astype(BF16)
    scaled = lax.all_to_all(
        jnp.broadcast_to(scaled[None], (tp, share, slots)), "tp", 0, 0, tiled=True
    ).reshape(1, rank, slots)
    spread = jnp.where(mine, scaled, jnp.zeros((), BF16)).reshape(per_group * rank, slots)
    delta = lax.dot_general(
        spread, adapter_up.reshape(per_group * rank, ho), (((0,), (0,)), ((), ())), preferred_element_type=F32
    ).astype(BF16)
    delta = lax.all_to_all(delta.reshape(groups, owner_slots, ho), "group", 0, 0, tiled=True)
    return lax.dot_general(
        place, delta.reshape(slots, ho), (((0,), (0,)), ((), ())), preferred_element_type=F32
    ).astype(BF16)


def solution(mesh):
    groups, tp = mesh.shape["group"], mesh.shape["tp"]

    def on_device(tokens, w_query, adapter_down, adapter_up, adapter_id):
        gathered = lax.all_gather(tokens, "tp", axis=1, tiled=True)
        delta = lora(tokens, adapter_down, adapter_up, adapter_id, groups, tp)
        base = jnp.dot(gathered, w_query, preferred_element_type=F32)
        return (base + delta.astype(F32)).astype(BF16)

    placed = (
        P("group", "tp"),
        P(None, "tp"),
        P("group", None, "tp"),
        P("group", None, "tp"),
        P("group"),
    )
    return jax.shard_map(
        on_device, mesh=mesh, in_specs=placed, out_specs=P("group", "tp"), check_vma=False
    )
```

```python
import jax
import jax.numpy as jnp
from jax import lax
from jax.experimental import pallas as pl
from jax.experimental.pallas import tpu as pltpu
from jax.sharding import PartitionSpec as P

adapter_scale_factor = 2.0
owner_slots = 48
F32, BF16 = jnp.float32, jnp.bfloat16


def slot_of_request(adapter_id, groups, per_group):
    n = adapter_id.shape[0]
    owner = adapter_id // per_group
    to_owner = owner[:, None] == lax.broadcasted_iota(jnp.int32, (n, groups), 1)
    before = lax.broadcasted_iota(jnp.int32, (n, n), 0) > lax.broadcasted_iota(jnp.int32, (n, n), 1)
    count = jnp.dot(before.astype(BF16), to_owner.astype(BF16), preferred_element_type=F32)
    rank = jnp.sum(jnp.where(to_owner, count, 0.0), axis=1).astype(jnp.int32)
    return owner * owner_slots + rank


def outgoing(tokens, adapter_id, groups, per_group):
    n, d = tokens.shape
    slots = groups * owner_slots
    slot = slot_of_request(adapter_id, groups, per_group)
    place = (lax.broadcasted_iota(jnp.int32, (slots, n), 0) == slot[None, :]).astype(BF16)
    rows = jnp.dot(place, tokens, preferred_element_type=F32).astype(BF16)
    local = (adapter_id % per_group).astype(BF16)
    ids = jnp.dot(place, local[:, None], preferred_element_type=F32).astype(BF16)
    ids = jnp.pad(ids.reshape(groups, 1, owner_slots), ((0, 0), (0, 7), (0, d - owner_slots)))
    return jnp.concatenate([rows.reshape(groups, owner_slots, d), ids], axis=1), place


def lora(here, place, adapter_down, adapter_up, groups, tp):
    per_group, rank, d = adapter_down.shape
    ho = adapter_up.shape[2]
    slots = groups * owner_slots
    rows = here[:, :owner_slots].reshape(slots, d)
    ids = here[:, owner_slots, :owner_slots].astype(jnp.int32).reshape(1, 1, slots)
    mine = lax.broadcasted_iota(jnp.int32, (per_group, 1, slots), 0) == ids
    part = lax.dot_general(
        adapter_down.reshape(per_group * rank, d), rows, (((1,), (1,)), ((), ())), preferred_element_type=F32
    ).reshape(per_group, rank, slots)
    part = jnp.sum(jnp.where(mine, part, 0.0), axis=0)
    share = rank // tp
    part = lax.all_to_all(part.reshape(tp, share, slots), "tp", 0, 0, tiled=True)
    scaled = (adapter_scale_factor * jnp.sum(part, axis=0)).astype(BF16)
    scaled = lax.all_to_all(
        jnp.broadcast_to(scaled[None], (tp, share, slots)), "tp", 0, 0, tiled=True
    ).reshape(1, rank, slots)
    spread = jnp.where(mine, scaled, jnp.zeros((), BF16)).reshape(per_group * rank, slots)
    delta = lax.dot_general(
        spread, adapter_up.reshape(per_group * rank, ho), (((0,), (0,)), ((), ())), preferred_element_type=F32
    ).astype(BF16)
    delta = lax.all_to_all(delta.reshape(groups, owner_slots, ho), "group", 0, 0, tiled=True)
    return lax.dot_general(
        place, delta.reshape(slots, ho), (((0,), (0,)), ((), ())), preferred_element_type=F32
    ).astype(BF16)


def partial_kernel(tok_a, tok_b, w_a, w_b, out):
    depth = tok_a.shape[1]
    cols = out.shape[2]
    acc = jnp.dot(tok_a[...], w_a[...].reshape(depth, cols), preferred_element_type=F32)
    acc += jnp.dot(tok_b[...], w_b[...].reshape(depth, cols), preferred_element_type=F32)
    out[0] = acc.astype(out.dtype)


def partials(tok_a, tok_b, w_a, w_b):
    n, depth = tok_a.shape
    chips, tp, r, cols = w_a.shape
    tok_spec = pl.BlockSpec((n, depth), lambda q: (0, 0))
    w_spec = pl.BlockSpec((chips, 1, r, cols), lambda q: (0, q, 0, 0))
    return pl.pallas_call(
        partial_kernel,
        grid=(tp,),
        in_specs=[tok_spec, tok_spec, w_spec, w_spec],
        out_specs=pl.BlockSpec((1, n, cols), lambda q: (q, 0, 0)),
        out_shape=jax.ShapeDtypeStruct((tp, n, cols), BF16),
        compiler_params=pltpu.CompilerParams(dimension_semantics=("arbitrary",)),
        name="partials",
    )(tok_a, tok_b, w_a, w_b)


def solution(mesh):
    groups, tp = mesh.shape["group"], mesh.shape["tp"]
    chips = groups // 2
    same_core = [[2 * chip + core for chip in range(chips)] for core in range(2)]
    other_core = [(g, g ^ 1) for g in range(groups)]

    def on_device(tokens, w_query, adapter_down, adapter_up, adapter_id):
        n, depth = tokens.shape
        cols = w_query.shape[1]
        r = depth // groups
        me = lax.axis_index("group")
        core, chip = me % 2, me // 2
        w_mine = lax.dynamic_index_in_dim(
            w_query.reshape(tp, groups, r, cols), core * chips + chip, 1, keepdims=False
        )
        w_mine = lax.all_to_all(w_mine, "tp", 0, 0, tiled=True)
        w_half = lax.all_to_all(
            jnp.broadcast_to(w_mine[None], (chips, tp, r, cols)), "group", 0, 0, axis_index_groups=same_core, tiled=True
        )
        sent, place = outgoing(tokens, adapter_id, groups, adapter_down.shape[0])
        w_half, sent = lax.optimization_barrier((w_half, sent))
        w_other = lax.ppermute(w_half, "group", other_core)
        here = lax.all_to_all(sent, "group", 0, 0, tiled=True)
        half = depth // 2
        tok_half = lax.dynamic_slice_in_dim(tokens, core * half, half, 1)
        tok_other = lax.dynamic_slice_in_dim(tokens, (1 - core) * half, half, 1)
        part = partials(tok_half, tok_other, w_half, w_other)
        base = lax.psum_scatter(part, "tp", scatter_dimension=0, tiled=False)
        delta = lora(here, place, adapter_down, adapter_up, groups, tp)
        return (base.astype(F32) + delta.astype(F32)).astype(BF16)

    placed = (
        P("group", "tp"),
        P(None, "tp"),
        P("group", None, "tp"),
        P("group", None, "tp"),
        P("group"),
    )
    return jax.shard_map(
        on_device, mesh=mesh, in_specs=placed, out_specs=P("group", "tp"), check_vma=False
    )
```

```python
import jax
import jax.numpy as jnp
from jax import lax
from jax.sharding import PartitionSpec as P

adapter_scale_factor = 2.0
owner_slots = 48
F32, BF16 = jnp.float32, jnp.bfloat16


def slot_of_request(adapter_id, groups, per_group):
    n = adapter_id.shape[0]
    owner = adapter_id // per_group
    to_owner = owner[:, None] == lax.broadcasted_iota(jnp.int32, (n, groups), 1)
    before = lax.broadcasted_iota(jnp.int32, (n, n), 0) > lax.broadcasted_iota(jnp.int32, (n, n), 1)
    count = jnp.dot(before.astype(BF16), to_owner.astype(BF16), preferred_element_type=F32)
    rank = jnp.sum(jnp.where(to_owner, count, 0.0), axis=1).astype(jnp.int32)
    return owner * owner_slots + rank


def outgoing(tokens, adapter_id, groups, per_group):
    n, d = tokens.shape
    slots = groups * owner_slots
    slot = slot_of_request(adapter_id, groups, per_group)
    place = (lax.broadcasted_iota(jnp.int32, (slots, n), 0) == slot[None, :]).astype(BF16)
    rows = jnp.dot(place, tokens, preferred_element_type=F32).astype(BF16)
    local = (adapter_id % per_group).astype(BF16)
    ids = jnp.dot(place, local[:, None], preferred_element_type=F32).astype(BF16)
    ids = jnp.pad(ids.reshape(groups, 1, owner_slots), ((0, 0), (0, 7), (0, d - owner_slots)))
    return jnp.concatenate([rows.reshape(groups, owner_slots, d), ids], axis=1), place


def lora(sent, place, at, adapter_down, adapter_up, groups, tp):
    per_group, rank, d = adapter_down.shape
    ho = adapter_up.shape[2]
    slots = groups * owner_slots
    here = lax.all_to_all(at(0, sent), "group", 0, 0, tiled=True)
    here = at(2, here)
    rows = here[:, :owner_slots].reshape(slots, d)
    ids = here[:, owner_slots, :owner_slots].astype(jnp.int32).reshape(1, 1, slots)
    mine = lax.broadcasted_iota(jnp.int32, (per_group, 1, slots), 0) == ids
    part = lax.dot_general(
        adapter_down.reshape(per_group * rank, d), rows, (((1,), (1,)), ((), ())), preferred_element_type=F32
    ).reshape(per_group, rank, slots)
    part = jnp.sum(jnp.where(mine, part, 0.0), axis=0)
    share = rank // tp
    part = lax.all_to_all(part.reshape(tp, share, slots), "tp", 0, 0, tiled=True)
    part = at(4, part)
    scaled = (adapter_scale_factor * jnp.sum(part, axis=0)).astype(BF16)
    scaled = lax.all_to_all(
        jnp.broadcast_to(scaled[None], (tp, share, slots)), "tp", 0, 0, tiled=True
    )
    scaled = at(6, scaled).reshape(1, rank, slots)
    spread = jnp.where(mine, scaled, jnp.zeros((), BF16)).reshape(per_group * rank, slots)
    delta = lax.dot_general(
        spread, adapter_up.reshape(per_group * rank, ho), (((0,), (0,)), ((), ())), preferred_element_type=F32
    ).astype(BF16)
    delta = lax.all_to_all(delta.reshape(groups, owner_slots, ho), "group", 0, 0, tiled=True)
    return lax.dot_general(
        place, delta.reshape(slots, ho), (((0,), (0,)), ((), ())), preferred_element_type=F32
    ).astype(BF16)


def solution(mesh):
    groups, tp = mesh.shape["group"], mesh.shape["tp"]
    right = [(z, (z + 1) % tp) for z in range(tp)]
    left = [(z, (z - 1) % tp) for z in range(tp)]

    def on_device(tokens, w_query, adapter_down, adapter_up, adapter_id):
        n, depth = tokens.shape
        cols = w_query.shape[1]
        z = lax.axis_index("tp")
        w = w_query.reshape(tp, depth, cols)

        def times_w(rows, owner):
            block = lax.dynamic_index_in_dim(w, owner % tp, 0, keepdims=False)
            return jnp.dot(rows, block, preferred_element_type=F32)

        from_left = [tokens]
        from_right = [tokens]
        for t in range(1, tp // 2):
            from_left.append(lax.ppermute(from_left[-1], "tp", right))
            from_right.append(lax.ppermute(from_right[-1], "tp", left))
        far = jnp.concatenate(
            [
                lax.ppermute(from_left[-1][: n // 2], "tp", right),
                lax.ppermute(from_right[-1][n // 2 :], "tp", left),
            ],
            axis=0,
        )
        base = times_w(tokens, z)
        for t in range(1, tp // 2):
            base += times_w(from_left[t], z + tp - t)
            base += times_w(from_right[t], z + t)
        base += times_w(far, z + tp // 2)

        def at(t, x):
            return lax.optimization_barrier((x, from_left[t]))[0]

        sent, place = outgoing(tokens, adapter_id, groups, adapter_down.shape[0])
        delta = lora(sent, place, at, adapter_down, adapter_up, groups, tp)
        return (base + delta.astype(F32)).astype(BF16)

    placed = (
        P("group", "tp"),
        P(None, "tp"),
        P("group", None, "tp"),
        P("group", None, "tp"),
        P("group"),
    )
    return jax.shard_map(
        on_device, mesh=mesh, in_specs=placed, out_specs=P("group", "tp"), check_vma=False
    )
```

```python
import jax
import jax.numpy as jnp
from jax import lax
from jax.experimental import pallas as pl
from jax.experimental.pallas import tpu as pltpu
from jax.sharding import PartitionSpec as P

adapter_scale_factor = 2.0
owner_slots = 48
F32, BF16 = jnp.float32, jnp.bfloat16


def slot_of_request(adapter_id, groups, per_group):
    n = adapter_id.shape[0]
    owner = adapter_id // per_group
    to_owner = owner[:, None] == lax.broadcasted_iota(jnp.int32, (n, groups), 1)
    before = lax.broadcasted_iota(jnp.int32, (n, n), 0) > lax.broadcasted_iota(jnp.int32, (n, n), 1)
    count = jnp.dot(before.astype(BF16), to_owner.astype(BF16), preferred_element_type=F32)
    rank = jnp.sum(jnp.where(to_owner, count, 0.0), axis=1).astype(jnp.int32)
    return owner * owner_slots + rank


def outgoing(tokens, adapter_id, groups, per_group):
    n, d = tokens.shape
    slots = groups * owner_slots
    slot = slot_of_request(adapter_id, groups, per_group)
    place = (lax.broadcasted_iota(jnp.int32, (slots, n), 0) == slot[None, :]).astype(BF16)
    rows = jnp.dot(place, tokens, preferred_element_type=F32).astype(BF16)
    local = (adapter_id % per_group).astype(BF16)
    ids = jnp.dot(place, local[:, None], preferred_element_type=F32).astype(BF16)
    ids = jnp.pad(ids.reshape(groups, 1, owner_slots), ((0, 0), (0, 7), (0, d - owner_slots)))
    return jnp.concatenate([rows.reshape(groups, owner_slots, d), ids], axis=1), place


def lora(here, place, adapter_down, adapter_up, groups):
    per_group, rank, d = adapter_down.shape
    ho = adapter_up.shape[2]
    slots = groups * owner_slots
    rows = here[:, :owner_slots].reshape(slots, d)
    ids = here[:, owner_slots, :owner_slots].astype(jnp.int32).reshape(1, 1, slots)
    mine = lax.broadcasted_iota(jnp.int32, (per_group, 1, slots), 0) == ids
    part = lax.dot_general(
        adapter_down.reshape(per_group * rank, d), rows, (((1,), (1,)), ((), ())), preferred_element_type=F32
    ).reshape(per_group, rank, slots)
    part = jnp.sum(jnp.where(mine, part, 0.0), axis=0)
    part = lax.all_gather(part.astype(BF16), "tp", axis=0, tiled=False)
    scaled = (adapter_scale_factor * jnp.sum(part.astype(F32), axis=0)).astype(BF16)[None]
    spread = jnp.where(mine, scaled, jnp.zeros((), BF16)).reshape(per_group * rank, slots)
    delta = lax.dot_general(
        spread, adapter_up.reshape(per_group * rank, ho), (((0,), (0,)), ((), ())), preferred_element_type=F32
    ).astype(BF16)
    delta = lax.all_to_all(delta.reshape(groups, owner_slots, ho), "group", 0, 0, tiled=True)
    return lax.dot_general(
        place, delta.reshape(slots, ho), (((0,), (0,)), ((), ())), preferred_element_type=F32
    ).astype(BF16)


per_step = 4
gathered_share = 3


def partial_kernel(tok, w_a, w_b, out):
    half = tok.shape[1] // 2
    for i in range(out.shape[0]):
        w = jnp.concatenate([w_a[:, i].reshape(half, -1), w_b[:, i].reshape(half, -1)], axis=0)
        out[i] = jnp.dot(tok[...], w, preferred_element_type=F32).astype(out.dtype)


def partials(tok, w_a, w_b):
    n, depth = tok.shape
    chips, tp, r, cols = w_a.shape
    w_spec = pl.BlockSpec((chips, per_step, r, cols), lambda q: (0, q, 0, 0))
    return pl.pallas_call(
        partial_kernel,
        grid=(tp // per_step,),
        in_specs=[pl.BlockSpec((n, depth), lambda q: (0, 0)), w_spec, w_spec],
        out_specs=pl.BlockSpec((per_step, n, cols), lambda q: (q, 0, 0)),
        out_shape=jax.ShapeDtypeStruct((tp, n, cols), BF16),
        compiler_params=pltpu.CompilerParams(dimension_semantics=("arbitrary",)),
        name="partials",
    )(tok, w_a, w_b)


def solution(mesh):
    groups, tp = mesh.shape["group"], mesh.shape["tp"]
    chips = groups // 2
    same_core = [[2 * chip + core for chip in range(chips)] for core in range(2)]
    other_core = [(g, g ^ 1) for g in range(groups)]

    def on_device(tokens, w_query, adapter_down, adapter_up, adapter_id):
        n, depth = tokens.shape
        cols = w_query.shape[1]
        r = depth // groups
        half = depth // 2
        whole = n // gathered_share
        me = lax.axis_index("group")
        core, chip = me % 2, me // 2
        gathered = lax.all_gather(tokens[:whole], "tp", axis=0, tiled=False)
        w_mine = lax.dynamic_index_in_dim(
            w_query.reshape(tp, groups, r, cols), core * chips + chip, 1, keepdims=False
        )
        w_mine = lax.all_to_all(w_mine, "tp", 0, 0, tiled=True)
        w_own = lax.all_to_all(
            jnp.broadcast_to(w_mine[None], (chips, tp, r, cols)), "group", 0, 0, axis_index_groups=same_core, tiled=True
        )
        sent, place = outgoing(tokens, adapter_id, groups, adapter_down.shape[0])
        tok = jnp.concatenate(
            [
                lax.dynamic_slice_in_dim(tokens[whole:], core * half, half, 1),
                lax.dynamic_slice_in_dim(tokens[whole:], (1 - core) * half, half, 1),
            ],
            axis=1,
        )
        w_own, sent, tok = lax.optimization_barrier((w_own, sent, tok))
        w_other = lax.ppermute(w_own, "group", other_core)
        here = lax.all_to_all(sent, "group", 0, 0, tiled=True)
        part = partials(tok, w_own, w_other)
        base = lax.psum_scatter(part, "tp", scatter_dimension=0, tiled=False)
        here, gathered, _ = lax.optimization_barrier((here, gathered, part))
        first = jnp.einsum(
            "znd,zdh->nh", gathered, w_query.reshape(tp, depth, cols), preferred_element_type=F32
        )
        delta = lora(here, place, adapter_down, adapter_up, groups).astype(F32)
        return jnp.concatenate(
            [(first + delta[:whole]).astype(BF16), (base.astype(F32) + delta[whole:]).astype(BF16)], axis=0
        )

    placed = (
        P("group", "tp"),
        P(None, "tp"),
        P("group", None, "tp"),
        P("group", None, "tp"),
        P("group"),
    )
    return jax.shard_map(
        on_device, mesh=mesh, in_specs=placed, out_specs=P("group", "tp"), check_vma=False
    )
```

```python
import jax
import jax.numpy as jnp
from jax import lax
from jax.sharding import PartitionSpec as P

adapter_scale_factor = 2.0
owner_slots = 48
ring_share = 3
F32, BF16 = jnp.float32, jnp.bfloat16


def slot_of_request(adapter_id, groups, per_group):
    n = adapter_id.shape[0]
    owner = adapter_id // per_group
    to_owner = owner[:, None] == lax.broadcasted_iota(jnp.int32, (n, groups), 1)
    before = lax.broadcasted_iota(jnp.int32, (n, n), 0) > lax.broadcasted_iota(jnp.int32, (n, n), 1)
    count = jnp.dot(before.astype(BF16), to_owner.astype(BF16), preferred_element_type=F32)
    rank = jnp.sum(jnp.where(to_owner, count, 0.0), axis=1).astype(jnp.int32)
    return owner * owner_slots + rank


def outgoing(tokens, adapter_id, groups, per_group):
    n, d = tokens.shape
    slots = groups * owner_slots
    slot = slot_of_request(adapter_id, groups, per_group)
    place = (lax.broadcasted_iota(jnp.int32, (slots, n), 0) == slot[None, :]).astype(BF16)
    rows = jnp.dot(place, tokens, preferred_element_type=F32).astype(BF16)
    local = (adapter_id % per_group).astype(BF16)
    ids = jnp.dot(place, local[:, None], preferred_element_type=F32).astype(BF16)
    ids = jnp.pad(ids.reshape(groups, 1, owner_slots), ((0, 0), (0, 7), (0, d - owner_slots)))
    return jnp.concatenate([rows.reshape(groups, owner_slots, d), ids], axis=1), place


def lora(sent, place, at, adapter_down, adapter_up, groups, tp):
    per_group, rank, d = adapter_down.shape
    ho = adapter_up.shape[2]
    slots = groups * owner_slots
    here = lax.all_to_all(at(0, sent), "group", 0, 0, tiled=True)
    here = at(2, here)
    rows = here[:, :owner_slots].reshape(slots, d)
    ids = here[:, owner_slots, :owner_slots].astype(jnp.int32).reshape(1, 1, slots)
    mine = lax.broadcasted_iota(jnp.int32, (per_group, 1, slots), 0) == ids
    part = lax.dot_general(
        adapter_down.reshape(per_group * rank, d), rows, (((1,), (1,)), ((), ())), preferred_element_type=F32
    ).reshape(per_group, rank, slots)
    part = jnp.sum(jnp.where(mine, part, 0.0), axis=0)
    share = rank // tp
    part = lax.all_to_all(part.reshape(tp, share, slots), "tp", 0, 0, tiled=True)
    part = at(4, part)
    scaled = (adapter_scale_factor * jnp.sum(part, axis=0)).astype(BF16)
    scaled = lax.all_to_all(
        jnp.broadcast_to(scaled[None], (tp, share, slots)), "tp", 0, 0, tiled=True
    )
    scaled = at(6, scaled).reshape(1, rank, slots)
    spread = jnp.where(mine, scaled, jnp.zeros((), BF16)).reshape(per_group * rank, slots)
    delta = lax.dot_general(
        spread, adapter_up.reshape(per_group * rank, ho), (((0,), (0,)), ((), ())), preferred_element_type=F32
    ).astype(BF16)
    delta = lax.all_to_all(delta.reshape(groups, owner_slots, ho), "group", 0, 0, tiled=True)
    return lax.dot_general(
        place, delta.reshape(slots, ho), (((0,), (0,)), ((), ())), preferred_element_type=F32
    ).astype(BF16)


def solution(mesh):
    groups, tp = mesh.shape["group"], mesh.shape["tp"]
    right = [(z, (z + 1) % tp) for z in range(tp)]
    left = [(z, (z - 1) % tp) for z in range(tp)]

    def on_device(tokens, w_query, adapter_down, adapter_up, adapter_id):
        n, depth = tokens.shape
        cols = w_query.shape[1]
        z = lax.axis_index("tp")
        w = w_query.reshape(tp, depth, cols)

        def times_w(rows, owner):
            block = lax.dynamic_index_in_dim(w, owner % tp, 0, keepdims=False)
            return jnp.dot(rows, block, preferred_element_type=F32)

        whole = n - n // ring_share
        gathered = lax.all_gather(tokens[:whole], "tp", axis=1, tiled=True)
        ring = tokens[whole:]
        n = n - whole
        from_left = [ring]
        from_right = [ring]
        for t in range(1, tp // 2):
            from_left.append(lax.ppermute(from_left[-1], "tp", right))
            from_right.append(lax.ppermute(from_right[-1], "tp", left))
        far = jnp.concatenate(
            [
                lax.ppermute(from_left[-1][: n // 2], "tp", right),
                lax.ppermute(from_right[-1][n // 2 :], "tp", left),
            ],
            axis=0,
        )
        base = times_w(ring, z)
        for t in range(1, tp // 2):
            base += times_w(from_left[t], z + tp - t)
            base += times_w(from_right[t], z + t)
        base += times_w(far, z + tp // 2)

        def at(t, x):
            return lax.optimization_barrier((x, from_left[t]))[0]

        sent, place = outgoing(tokens, adapter_id, groups, adapter_down.shape[0])
        delta = lora(sent, place, at, adapter_down, adapter_up, groups, tp)
        delta, base, gathered = lax.optimization_barrier((delta, base, gathered))
        first = jnp.dot(gathered, w_query, preferred_element_type=F32) + delta[:whole].astype(F32)
        base += delta[whole:].astype(F32)
        return jnp.concatenate([first.astype(BF16), base.astype(BF16)], axis=0)

    placed = (
        P("group", "tp"),
        P(None, "tp"),
        P("group", None, "tp"),
        P("group", None, "tp"),
        P("group"),
    )
    return jax.shard_map(
        on_device, mesh=mesh, in_specs=placed, out_specs=P("group", "tp"), check_vma=False
    )
```

```python
import jax
import jax.numpy as jnp
from jax import lax
from jax.experimental import pallas as pl
from jax.experimental.pallas import tpu as pltpu
from jax.sharding import PartitionSpec as P

adapter_scale_factor = 2.0
owner_slots = 48
F32, BF16 = jnp.float32, jnp.bfloat16


def slot_of_request(adapter_id, groups, per_group):
    n = adapter_id.shape[0]
    owner = adapter_id // per_group
    to_owner = owner[:, None] == lax.broadcasted_iota(jnp.int32, (n, groups), 1)
    before = lax.broadcasted_iota(jnp.int32, (n, n), 0) > lax.broadcasted_iota(jnp.int32, (n, n), 1)
    count = jnp.dot(before.astype(BF16), to_owner.astype(BF16), preferred_element_type=F32)
    rank = jnp.sum(jnp.where(to_owner, count, 0.0), axis=1).astype(jnp.int32)
    return owner * owner_slots + rank


def lora(tokens, adapter_down, adapter_up, adapter_id, groups, tp):
    n, d = tokens.shape
    per_group, rank, _ = adapter_down.shape
    ho = adapter_up.shape[2]
    slots = groups * owner_slots
    slot = slot_of_request(adapter_id, groups, per_group)
    place = (lax.broadcasted_iota(jnp.int32, (slots, n), 0) == slot[None, :]).astype(BF16)
    out_rows = jnp.dot(place, tokens, preferred_element_type=F32).astype(BF16)
    local = (adapter_id % per_group).astype(BF16)
    out_ids = jnp.dot(place, local[:, None], preferred_element_type=F32).astype(BF16)
    out_ids = out_ids.reshape(groups, 1, owner_slots)
    out_ids = jnp.pad(out_ids, ((0, 0), (0, 7), (0, d - owner_slots)))
    sent = jnp.concatenate([out_rows.reshape(groups, owner_slots, d), out_ids], axis=1)
    here = lax.all_to_all(sent, "group", 0, 0, tiled=True)
    rows = here[:, :owner_slots].reshape(slots, d)
    ids = here[:, owner_slots, :owner_slots].astype(jnp.int32).reshape(1, 1, slots)
    mine = lax.broadcasted_iota(jnp.int32, (per_group, 1, slots), 0) == ids
    part = lax.dot_general(
        adapter_down.reshape(per_group * rank, d), rows, (((1,), (1,)), ((), ())), preferred_element_type=F32
    ).reshape(per_group, rank, slots)
    part = jnp.sum(jnp.where(mine, part, 0.0), axis=0)
    share = rank // tp
    part = lax.all_to_all(part.reshape(tp, share, slots), "tp", 0, 0, tiled=True)
    scaled = (adapter_scale_factor * jnp.sum(part, axis=0)).astype(BF16)
    scaled = lax.all_to_all(
        jnp.broadcast_to(scaled[None], (tp, share, slots)), "tp", 0, 0, tiled=True
    ).reshape(1, rank, slots)
    spread = jnp.where(mine, scaled, jnp.zeros((), BF16)).reshape(per_group * rank, slots)
    delta = lax.dot_general(
        spread, adapter_up.reshape(per_group * rank, ho), (((0,), (0,)), ((), ())), preferred_element_type=F32
    ).astype(BF16)
    delta = lax.all_to_all(delta.reshape(groups, owner_slots, ho), "group", 0, 0, tiled=True)
    return lax.dot_general(
        place, delta.reshape(slots, ho), (((0,), (0,)), ((), ())), preferred_element_type=F32
    ).astype(BF16)


def query_kernel(tok, w, delta, out):
    base = jnp.dot(tok[...], w[...], preferred_element_type=F32)
    rows = tok.shape[0]
    at = pl.ds(pl.multiple_of(pl.program_id(0) * rows, rows), rows)
    out[...] = (base + delta[at, :].astype(F32)).astype(out.dtype)


def query_of(tokens, w, delta):
    n, d = tokens.shape
    cols = w.shape[1]
    rows = n // 4
    return pl.pallas_call(
        query_kernel,
        grid=(n // rows,),
        in_specs=[
            pl.BlockSpec((rows, d), lambda i: (i, 0)),
            pl.BlockSpec(memory_space=pltpu.VMEM),
            pl.BlockSpec(memory_space=pltpu.VMEM),
        ],
        out_specs=pl.BlockSpec((rows, cols), lambda i: (i, 0)),
        out_shape=jax.ShapeDtypeStruct((n, cols), BF16),
        compiler_params=pltpu.CompilerParams(dimension_semantics=("arbitrary",)),
        name="query",
    )(tokens, w, delta)


def solution(mesh):
    groups, tp = mesh.shape["group"], mesh.shape["tp"]

    def on_device(tokens, w_query, adapter_down, adapter_up, adapter_id):
        gathered = lax.all_gather(tokens, "tp", axis=1, tiled=True)
        delta = lora(tokens, adapter_down, adapter_up, adapter_id, groups, tp)
        return query_of(gathered, w_query, delta)

    placed = (
        P("group", "tp"),
        P(None, "tp"),
        P("group", None, "tp"),
        P("group", None, "tp"),
        P("group"),
    )
    return jax.shard_map(
        on_device, mesh=mesh, in_specs=placed, out_specs=P("group", "tp"), check_vma=False
    )
```

```python
import jax
import jax.numpy as jnp
from jax import lax
from jax.experimental import pallas as pl
from jax.experimental.pallas import tpu as pltpu
from jax.sharding import PartitionSpec as P

adapter_scale_factor = 2.0
owner_slots = 48
F32, BF16 = jnp.float32, jnp.bfloat16


def slot_of_request(adapter_id, groups, per_group):
    n = adapter_id.shape[0]
    owner = adapter_id // per_group
    to_owner = owner[:, None] == lax.broadcasted_iota(jnp.int32, (n, groups), 1)
    before = lax.broadcasted_iota(jnp.int32, (n, n), 0) > lax.broadcasted_iota(jnp.int32, (n, n), 1)
    count = jnp.dot(before.astype(BF16), to_owner.astype(BF16), preferred_element_type=F32)
    rank = jnp.sum(jnp.where(to_owner, count, 0.0), axis=1).astype(jnp.int32)
    return owner * owner_slots + rank


def lora(tokens, adapter_down, adapter_up, adapter_id, groups, tp):
    n, d = tokens.shape
    per_group, rank, _ = adapter_down.shape
    ho = adapter_up.shape[2]
    slots = groups * owner_slots
    slot = slot_of_request(adapter_id, groups, per_group)
    place = (lax.broadcasted_iota(jnp.int32, (slots, n), 0) == slot[None, :]).astype(BF16)
    out_rows = jnp.dot(place, tokens, preferred_element_type=F32).astype(BF16)
    local = (adapter_id % per_group).astype(BF16)
    out_ids = jnp.dot(place, local[:, None], preferred_element_type=F32).astype(BF16)
    out_ids = out_ids.reshape(groups, 1, owner_slots)
    out_ids = jnp.pad(out_ids, ((0, 0), (0, 7), (0, d - owner_slots)))
    sent = jnp.concatenate([out_rows.reshape(groups, owner_slots, d), out_ids], axis=1)
    here = lax.all_to_all(sent, "group", 0, 0, tiled=True)
    rows = here[:, :owner_slots].reshape(slots, d)
    ids = here[:, owner_slots, :owner_slots].astype(jnp.int32).reshape(1, 1, slots)
    mine = lax.broadcasted_iota(jnp.int32, (per_group, 1, slots), 0) == ids
    part = lax.dot_general(
        adapter_down.reshape(per_group * rank, d), rows, (((1,), (1,)), ((), ())), preferred_element_type=F32
    ).reshape(per_group, rank, slots)
    part = jnp.sum(jnp.where(mine, part, 0.0), axis=0)
    share = rank // tp
    part = lax.all_to_all(part.reshape(tp, share, slots), "tp", 0, 0, tiled=True)
    scaled = (adapter_scale_factor * jnp.sum(part, axis=0)).astype(BF16)
    scaled = lax.all_to_all(
        jnp.broadcast_to(scaled[None], (tp, share, slots)), "tp", 0, 0, tiled=True
    ).reshape(1, rank, slots)
    spread = jnp.where(mine, scaled, jnp.zeros((), BF16)).reshape(per_group * rank, slots)
    delta = lax.dot_general(
        spread, adapter_up.reshape(per_group * rank, ho), (((0,), (0,)), ((), ())), preferred_element_type=F32
    ).astype(BF16)
    delta = lax.all_to_all(delta.reshape(groups, owner_slots, ho), "group", 0, 0, tiled=True)
    return lax.dot_general(
        place, delta.reshape(slots, ho), (((0,), (0,)), ((), ())), preferred_element_type=F32
    ).astype(BF16)


chunks = 8


def query_kernel(tok, w, delta, out, held, held_w, sems, sems_w):
    depth = held.shape[2]
    copies = []
    for k in range(chunks):
        part = pl.ds(k * depth, depth)
        copies.append(pltpu.make_async_copy(tok.at[:, part], held.at[k], sems.at[k]))
        copies.append(pltpu.make_async_copy(w.at[part, :], held_w.at[k], sems_w.at[k]))
    for copy in copies:
        copy.start()
    base = delta[...].astype(F32)
    for k in range(chunks):
        copies[2 * k].wait()
        copies[2 * k + 1].wait()
        base += jnp.dot(held[k], held_w[k], preferred_element_type=F32)
    out[...] = base.astype(out.dtype)


def query_of(tokens, w, delta):
    n, d = tokens.shape
    cols = w.shape[1]
    vmem, far = pl.BlockSpec(memory_space=pltpu.VMEM), pl.BlockSpec(memory_space=pl.ANY)
    return pl.pallas_call(
        query_kernel,
        in_specs=[far, far, vmem],
        out_specs=vmem,
        out_shape=jax.ShapeDtypeStruct((n, cols), BF16),
        scratch_shapes=[
            pltpu.VMEM((chunks, n, d // chunks), BF16),
            pltpu.VMEM((chunks, d // chunks, cols), BF16),
            pltpu.SemaphoreType.DMA((chunks,)),
            pltpu.SemaphoreType.DMA((chunks,)),
        ],
        compiler_params=pltpu.CompilerParams(vmem_limit_bytes=60 * 1024 * 1024),
        name="query",
    )(tokens, w, delta)


def solution(mesh):
    groups, tp = mesh.shape["group"], mesh.shape["tp"]

    def on_device(tokens, w_query, adapter_down, adapter_up, adapter_id):
        gathered = lax.all_gather(tokens, "tp", axis=1, tiled=True)
        delta = lora(tokens, adapter_down, adapter_up, adapter_id, groups, tp)
        return query_of(gathered, w_query, delta)

    placed = (
        P("group", "tp"),
        P(None, "tp"),
        P("group", None, "tp"),
        P("group", None, "tp"),
        P("group"),
    )
    return jax.shard_map(
        on_device, mesh=mesh, in_specs=placed, out_specs=P("group", "tp"), check_vma=False
    )
```

```python
import jax
import jax.numpy as jnp
from jax import lax
from jax.experimental import pallas as pl
from jax.experimental.pallas import tpu as pltpu
from jax.sharding import PartitionSpec as P

adapter_scale_factor = 2.0
owner_slots = 48
F32, BF16 = jnp.float32, jnp.bfloat16


def slot_of_request(adapter_id, groups, per_group):
    n = adapter_id.shape[0]
    owner = adapter_id // per_group
    to_owner = owner[:, None] == lax.broadcasted_iota(jnp.int32, (n, groups), 1)
    before = lax.broadcasted_iota(jnp.int32, (n, n), 0) > lax.broadcasted_iota(jnp.int32, (n, n), 1)
    count = jnp.dot(before.astype(BF16), to_owner.astype(BF16), preferred_element_type=F32)
    rank = jnp.sum(jnp.where(to_owner, count, 0.0), axis=1).astype(jnp.int32)
    return owner * owner_slots + rank


def lora(tokens, adapter_down, adapter_up, adapter_id, groups, tp):
    n, d = tokens.shape
    per_group, rank, _ = adapter_down.shape
    ho = adapter_up.shape[2]
    slots = groups * owner_slots
    slot = slot_of_request(adapter_id, groups, per_group)
    place = (lax.broadcasted_iota(jnp.int32, (slots, n), 0) == slot[None, :]).astype(BF16)
    out_rows = jnp.dot(place, tokens, preferred_element_type=F32).astype(BF16)
    local = (adapter_id % per_group).astype(BF16)
    out_ids = jnp.dot(place, local[:, None], preferred_element_type=F32).astype(BF16)
    out_ids = out_ids.reshape(groups, 1, owner_slots)
    out_ids = jnp.pad(out_ids, ((0, 0), (0, 7), (0, d - owner_slots)))
    sent = jnp.concatenate([out_rows.reshape(groups, owner_slots, d), out_ids], axis=1)
    here = lax.all_to_all(sent, "group", 0, 0, tiled=True)
    rows = here[:, :owner_slots].reshape(slots, d)
    ids = here[:, owner_slots, :owner_slots].astype(jnp.int32).reshape(1, 1, slots)
    mine = lax.broadcasted_iota(jnp.int32, (per_group, 1, slots), 0) == ids
    part = lax.dot_general(
        adapter_down.reshape(per_group * rank, d), rows, (((1,), (1,)), ((), ())), preferred_element_type=F32
    ).reshape(per_group, rank, slots)
    part = jnp.sum(jnp.where(mine, part, 0.0), axis=0)
    share = rank // tp
    part = lax.all_to_all(part.reshape(tp, share, slots), "tp", 0, 0, tiled=True)
    scaled = (adapter_scale_factor * jnp.sum(part, axis=0)).astype(BF16)
    scaled = lax.all_to_all(
        jnp.broadcast_to(scaled[None], (tp, share, slots)), "tp", 0, 0, tiled=True
    ).reshape(1, rank, slots)
    spread = jnp.where(mine, scaled, jnp.zeros((), BF16)).reshape(per_group * rank, slots)
    delta = lax.dot_general(
        spread, adapter_up.reshape(per_group * rank, ho), (((0,), (0,)), ((), ())), preferred_element_type=F32
    ).astype(BF16)
    delta = lax.all_to_all(delta.reshape(groups, owner_slots, ho), "group", 0, 0, tiled=True)
    return lax.dot_general(
        place, delta.reshape(slots, ho), (((0,), (0,)), ((), ())), preferred_element_type=F32
    ).astype(BF16)


chunk_parts = (1, 1, 2, 2, 2, 2, 2, 2, 2)


def query_kernel(tok, w, delta, out, held, held_w, sems, sems_w):
    unit = held.shape[1] // sum(chunk_parts)
    parts, copies, start = [], [], 0
    for k, size in enumerate(chunk_parts):
        part = pl.ds(start * unit, size * unit)
        start += size
        parts.append(part)
        copies.append(
            (
                pltpu.make_async_copy(tok.at[:, part], held.at[:, part], sems.at[k]),
                pltpu.make_async_copy(w.at[part, :], held_w.at[part, :], sems_w.at[k]),
            )
        )
    for pair in copies[:2]:
        for copy in pair:
            copy.start()
    base = delta[...].astype(F32)
    for k, part in enumerate(parts):
        for copy in copies[k]:
            copy.wait()
        if k + 2 < len(copies):
            for copy in copies[k + 2]:
                copy.start()
        base += jnp.dot(held[:, part], held_w[part, :], preferred_element_type=F32)
    out[...] = base.astype(out.dtype)


def query_of(tokens, w, delta):
    n, d = tokens.shape
    cols = w.shape[1]
    vmem, far = pl.BlockSpec(memory_space=pltpu.VMEM), pl.BlockSpec(memory_space=pl.ANY)
    return pl.pallas_call(
        query_kernel,
        in_specs=[far, far, vmem],
        out_specs=vmem,
        out_shape=jax.ShapeDtypeStruct((n, cols), BF16),
        scratch_shapes=[
            pltpu.VMEM((n, d), BF16),
            pltpu.VMEM((d, cols), BF16),
            pltpu.SemaphoreType.DMA((len(chunk_parts),)),
            pltpu.SemaphoreType.DMA((len(chunk_parts),)),
        ],
        compiler_params=pltpu.CompilerParams(vmem_limit_bytes=60 * 1024 * 1024),
        name="query",
    )(tokens, w, delta)


def solution(mesh):
    groups, tp = mesh.shape["group"], mesh.shape["tp"]

    def on_device(tokens, w_query, adapter_down, adapter_up, adapter_id):
        gathered = lax.all_gather(tokens, "tp", axis=1, tiled=True)
        delta = lora(tokens, adapter_down, adapter_up, adapter_id, groups, tp)
        return query_of(gathered, w_query, delta)

    placed = (
        P("group", "tp"),
        P(None, "tp"),
        P("group", None, "tp"),
        P("group", None, "tp"),
        P("group"),
    )
    return jax.shard_map(
        on_device, mesh=mesh, in_specs=placed, out_specs=P("group", "tp"), check_vma=False
    )
```

```python
import jax
import jax.numpy as jnp
from jax import lax
from jax.sharding import PartitionSpec as P

adapter_scale_factor = 2.0
owner_slots = 48
F32, BF16 = jnp.float32, jnp.bfloat16


def slot_of_request(adapter_id, groups, per_group):
    n = adapter_id.shape[0]
    owner = adapter_id // per_group
    to_owner = owner[:, None] == lax.broadcasted_iota(jnp.int32, (n, groups), 1)
    before = lax.broadcasted_iota(jnp.int32, (n, n), 0) > lax.broadcasted_iota(jnp.int32, (n, n), 1)
    count = jnp.dot(before.astype(BF16), to_owner.astype(BF16), preferred_element_type=F32)
    rank = jnp.sum(jnp.where(to_owner, count, 0.0), axis=1).astype(jnp.int32)
    return owner * owner_slots + rank


def lora(tokens, adapter_down, adapter_up, adapter_id, groups, tp):
    n, d = tokens.shape
    per_group, rank, _ = adapter_down.shape
    ho = adapter_up.shape[2]
    slots = groups * owner_slots
    slot = slot_of_request(adapter_id, groups, per_group)
    place = (lax.broadcasted_iota(jnp.int32, (slots, n), 0) == slot[None, :]).astype(BF16)
    out_rows = jnp.dot(place, tokens, preferred_element_type=F32).astype(BF16)
    local = (adapter_id % per_group).astype(BF16)
    out_ids = jnp.dot(place, local[:, None], preferred_element_type=F32).astype(BF16)
    out_ids = out_ids.reshape(groups, 1, owner_slots)
    out_ids = jnp.pad(out_ids, ((0, 0), (0, 7), (0, d - owner_slots)))
    sent = jnp.concatenate([out_rows.reshape(groups, owner_slots, d), out_ids], axis=1)
    here = lax.all_to_all(sent, "group", 0, 0, tiled=True)
    rows = here[:, :owner_slots].reshape(slots, d)
    ids = here[:, owner_slots, :owner_slots].astype(jnp.int32).reshape(1, 1, slots)
    mine = lax.broadcasted_iota(jnp.int32, (per_group, 1, slots), 0) == ids
    part = lax.dot_general(
        adapter_down.reshape(per_group * rank, d), rows, (((1,), (1,)), ((), ())), preferred_element_type=F32
    ).reshape(per_group, rank, slots)
    part = jnp.sum(jnp.where(mine, part, 0.0), axis=0)
    share = rank // tp
    part = lax.all_to_all(part.reshape(tp, share, slots), "tp", 0, 0, tiled=True)
    scaled = (adapter_scale_factor * jnp.sum(part, axis=0)).astype(BF16)
    scaled = lax.all_to_all(
        jnp.broadcast_to(scaled[None], (tp, share, slots)), "tp", 0, 0, tiled=True
    ).reshape(1, rank, slots)
    spread = jnp.where(mine, scaled, jnp.zeros((), BF16)).reshape(per_group * rank, slots)
    delta = lax.dot_general(
        spread, adapter_up.reshape(per_group * rank, ho), (((0,), (0,)), ((), ())), preferred_element_type=F32
    ).astype(BF16)
    delta = lax.all_to_all(delta.reshape(groups, owner_slots, ho), "group", 0, 0, tiled=True)
    return lax.dot_general(
        place, delta.reshape(slots, ho), (((0,), (0,)), ((), ())), preferred_element_type=F32
    ).astype(BF16)


def solution(mesh):
    groups, tp = mesh.shape["group"], mesh.shape["tp"]

    def on_device(tokens, w_query, adapter_down, adapter_up, adapter_id):
        gathered = lax.all_gather(tokens, "tp", axis=1, tiled=True)
        delta = lora(tokens, adapter_down, adapter_up, adapter_id, groups, tp)
        delta, gathered = lax.optimization_barrier((delta, gathered))
        base = lax.optimization_barrier(jnp.dot(gathered, w_query, preferred_element_type=F32))
        return (base + delta.astype(F32)).astype(BF16)

    placed = (
        P("group", "tp"),
        P(None, "tp"),
        P("group", None, "tp"),
        P("group", None, "tp"),
        P("group"),
    )
    return jax.shard_map(
        on_device, mesh=mesh, in_specs=placed, out_specs=P("group", "tp"), check_vma=False
    )
```

```python
import jax
import jax.numpy as jnp
from jax import lax
from jax.sharding import PartitionSpec as P

adapter_scale_factor = 2.0
owner_slots = 48
F32, BF16 = jnp.float32, jnp.bfloat16


def slot_of_request(adapter_id, groups, per_group):
    n = adapter_id.shape[0]
    owner = adapter_id // per_group
    to_owner = owner[:, None] == lax.broadcasted_iota(jnp.int32, (n, groups), 1)
    before = lax.broadcasted_iota(jnp.int32, (n, n), 0) > lax.broadcasted_iota(jnp.int32, (n, n), 1)
    count = jnp.dot(before.astype(BF16), to_owner.astype(BF16), preferred_element_type=F32)
    rank = jnp.sum(jnp.where(to_owner, count, 0.0), axis=1).astype(jnp.int32)
    return owner * owner_slots + rank


def lora(tokens, adapter_down, adapter_up, adapter_id, groups, tp):
    n, d = tokens.shape
    per_group, rank, _ = adapter_down.shape
    ho = adapter_up.shape[2]
    slots = groups * owner_slots
    slot = slot_of_request(adapter_id, groups, per_group)
    place = (lax.broadcasted_iota(jnp.int32, (slots, n), 0) == slot[None, :]).astype(BF16)
    out_rows = jnp.dot(place, tokens, preferred_element_type=F32).astype(BF16)
    local = (adapter_id % per_group).astype(BF16)
    out_ids = jnp.dot(place, local[:, None], preferred_element_type=F32).astype(BF16)
    out_ids = out_ids.reshape(groups, 1, owner_slots)
    out_ids = jnp.pad(out_ids, ((0, 0), (0, 7), (0, d - owner_slots)))
    sent = jnp.concatenate([out_rows.reshape(groups, owner_slots, d), out_ids], axis=1)
    here = lax.all_to_all(sent, "group", 0, 0, tiled=True)
    rows = here[:, :owner_slots].reshape(slots, d)
    ids = here[:, owner_slots, :owner_slots].astype(jnp.int32).reshape(1, 1, slots)
    mine = lax.broadcasted_iota(jnp.int32, (per_group, 1, slots), 0) == ids
    part = lax.dot_general(
        adapter_down.reshape(per_group * rank, d), rows, (((1,), (1,)), ((), ())), preferred_element_type=F32
    ).reshape(per_group, rank, slots)
    part = jnp.sum(jnp.where(mine, part, 0.0), axis=0)
    share = rank // tp
    part = lax.all_to_all(part.reshape(tp, share, slots), "tp", 0, 0, tiled=True)
    scaled = (adapter_scale_factor * jnp.sum(part, axis=0)).astype(BF16)
    scaled = lax.all_to_all(
        jnp.broadcast_to(scaled[None], (tp, share, slots)), "tp", 0, 0, tiled=True
    ).reshape(1, rank, slots)
    spread = jnp.where(mine, scaled, jnp.zeros((), BF16)).reshape(per_group * rank, slots)
    delta = lax.dot_general(
        spread, adapter_up.reshape(per_group * rank, ho), (((0,), (0,)), ((), ())), preferred_element_type=F32
    ).astype(BF16)
    delta = lax.all_to_all(delta.reshape(groups, owner_slots, ho), "group", 0, 0, tiled=True)
    return lax.dot_general(
        place, delta.reshape(slots, ho), (((0,), (0,)), ((), ())), preferred_element_type=F32
    ).astype(BF16)


def solution(mesh):
    groups, tp = mesh.shape["group"], mesh.shape["tp"]

    def on_device(tokens, w_query, adapter_down, adapter_up, adapter_id):
        gathered = lax.all_gather(tokens, "tp", axis=0, tiled=False)
        delta = lora(tokens, adapter_down, adapter_up, adapter_id, groups, tp)
        delta, gathered = lax.optimization_barrier((delta, gathered))
        base = lax.optimization_barrier(
            jnp.einsum(
                "znd,zdh->nh", gathered, w_query.reshape(gathered.shape[0], -1, w_query.shape[1]), preferred_element_type=F32
            )
        )
        return (base + delta.astype(F32)).astype(BF16)

    placed = (
        P("group", "tp"),
        P(None, "tp"),
        P("group", None, "tp"),
        P("group", None, "tp"),
        P("group"),
    )
    return jax.shard_map(
        on_device, mesh=mesh, in_specs=placed, out_specs=P("group", "tp"), check_vma=False
    )
```

```python
import jax
import jax.numpy as jnp
from jax import lax
from jax.sharding import PartitionSpec as P

adapter_scale_factor = 2.0
owner_slots = 48
F32, BF16 = jnp.float32, jnp.bfloat16


def slot_of_request(adapter_id, groups, per_group):
    n = adapter_id.shape[0]
    owner = adapter_id // per_group
    to_owner = owner[:, None] == lax.broadcasted_iota(jnp.int32, (n, groups), 1)
    before = lax.broadcasted_iota(jnp.int32, (n, n), 0) > lax.broadcasted_iota(jnp.int32, (n, n), 1)
    count = jnp.dot(before.astype(BF16), to_owner.astype(BF16), preferred_element_type=F32)
    rank = jnp.sum(jnp.where(to_owner, count, 0.0), axis=1).astype(jnp.int32)
    return owner * owner_slots + rank


def lora(tokens, adapter_down, adapter_up, adapter_id, groups, tp):
    n, d = tokens.shape
    per_group, rank, _ = adapter_down.shape
    ho = adapter_up.shape[2]
    slots = groups * owner_slots
    slot = slot_of_request(adapter_id, groups, per_group)
    place = (lax.broadcasted_iota(jnp.int32, (slots, n), 0) == slot[None, :]).astype(BF16)
    out_rows = jnp.dot(place, tokens, preferred_element_type=F32).astype(BF16)
    local = (adapter_id % per_group).astype(BF16)
    out_ids = jnp.dot(place, local[:, None], preferred_element_type=F32).astype(BF16)
    out_ids = out_ids.reshape(groups, 1, owner_slots)
    out_ids = jnp.pad(out_ids, ((0, 0), (0, 7), (0, d - owner_slots)))
    sent = jnp.concatenate([out_rows.reshape(groups, owner_slots, d), out_ids], axis=1)
    here = lax.all_to_all(sent, "group", 0, 0, tiled=True)
    rows = here[:, :owner_slots].reshape(slots, d)
    ids = here[:, owner_slots, :owner_slots].astype(jnp.int32).reshape(1, 1, slots)
    mine = lax.broadcasted_iota(jnp.int32, (per_group, 1, slots), 0) == ids
    part = lax.dot_general(
        adapter_down.reshape(per_group * rank, d), rows, (((1,), (1,)), ((), ())), preferred_element_type=F32
    ).reshape(per_group, rank, slots)
    part = jnp.sum(jnp.where(mine, part, 0.0), axis=0)
    share = rank // tp
    part = lax.all_to_all(part.astype(BF16).reshape(tp, share, slots), "tp", 0, 0, tiled=True)
    scaled = (adapter_scale_factor * jnp.sum(part.astype(F32), axis=0)).astype(BF16)
    scaled = lax.all_to_all(
        jnp.broadcast_to(scaled[None], (tp, share, slots)), "tp", 0, 0, tiled=True
    ).reshape(1, rank, slots)
    spread = jnp.where(mine, scaled, jnp.zeros((), BF16)).reshape(per_group * rank, slots)
    delta = lax.dot_general(
        spread, adapter_up.reshape(per_group * rank, ho), (((0,), (0,)), ((), ())), preferred_element_type=F32
    ).astype(BF16)
    delta = lax.all_to_all(delta.reshape(groups, owner_slots, ho), "group", 0, 0, tiled=True)
    return lax.dot_general(
        place, delta.reshape(slots, ho), (((0,), (0,)), ((), ())), preferred_element_type=F32
    ).astype(BF16)


def solution(mesh):
    groups, tp = mesh.shape["group"], mesh.shape["tp"]

    def on_device(tokens, w_query, adapter_down, adapter_up, adapter_id):
        gathered = lax.all_gather(tokens, "tp", axis=1, tiled=True)
        delta = lora(tokens, adapter_down, adapter_up, adapter_id, groups, tp)
        delta, gathered = lax.optimization_barrier((delta, gathered))
        base = lax.optimization_barrier(jnp.dot(gathered, w_query, preferred_element_type=F32))
        return (base + delta.astype(F32)).astype(BF16)

    placed = (
        P("group", "tp"),
        P(None, "tp"),
        P("group", None, "tp"),
        P("group", None, "tp"),
        P("group"),
    )
    return jax.shard_map(
        on_device, mesh=mesh, in_specs=placed, out_specs=P("group", "tp"), check_vma=False
    )
```

```python
import jax
import jax.numpy as jnp
from jax import lax
from jax.sharding import PartitionSpec as P

adapter_scale_factor = 2.0
owner_slots = 48
F32, BF16 = jnp.float32, jnp.bfloat16


def slot_of_request(adapter_id, groups, per_group):
    n = adapter_id.shape[0]
    owner = adapter_id // per_group
    to_owner = owner[:, None] == lax.broadcasted_iota(jnp.int32, (n, groups), 1)
    before = lax.broadcasted_iota(jnp.int32, (n, n), 0) > lax.broadcasted_iota(jnp.int32, (n, n), 1)
    count = jnp.dot(before.astype(BF16), to_owner.astype(BF16), preferred_element_type=F32)
    rank = jnp.sum(jnp.where(to_owner, count, 0.0), axis=1).astype(jnp.int32)
    return owner * owner_slots + rank


def lora(tokens, adapter_down, adapter_up, adapter_id, groups, tp):
    n, d = tokens.shape
    per_group, rank, _ = adapter_down.shape
    ho = adapter_up.shape[2]
    slots = groups * owner_slots
    slot = slot_of_request(adapter_id, groups, per_group)
    place = (lax.broadcasted_iota(jnp.int32, (slots, n), 0) == slot[None, :]).astype(BF16)
    out_rows = jnp.dot(place, tokens, preferred_element_type=F32).astype(BF16)
    local = (adapter_id % per_group).astype(BF16)
    out_ids = jnp.dot(place, local[:, None], preferred_element_type=F32).astype(jnp.int32)
    ids = lax.all_to_all(out_ids.reshape(groups, 1, owner_slots), "group", 0, 0, tiled=True).reshape(1, 1, slots)
    rows = lax.all_to_all(out_rows.reshape(groups, owner_slots, d), "group", 0, 0, tiled=True).reshape(slots, d)
    mine = lax.broadcasted_iota(jnp.int32, (per_group, 1, slots), 0) == ids
    part = lax.dot_general(
        adapter_down.reshape(per_group * rank, d), rows, (((1,), (1,)), ((), ())), preferred_element_type=F32
    ).reshape(per_group, rank, slots)
    part = jnp.sum(jnp.where(mine, part, 0.0), axis=0)
    share = rank // tp
    part = lax.all_to_all(part.astype(BF16).reshape(tp, share, slots), "tp", 0, 0, tiled=True)
    scaled = (adapter_scale_factor * jnp.sum(part.astype(F32), axis=0)).astype(BF16)
    scaled = lax.all_to_all(
        jnp.broadcast_to(scaled[None], (tp, share, slots)), "tp", 0, 0, tiled=True
    ).reshape(1, rank, slots)
    spread = jnp.where(mine, scaled, jnp.zeros((), BF16)).reshape(per_group * rank, slots)
    delta = lax.dot_general(
        spread, adapter_up.reshape(per_group * rank, ho), (((0,), (0,)), ((), ())), preferred_element_type=F32
    ).astype(BF16)
    delta = lax.all_to_all(delta.reshape(groups, owner_slots, ho), "group", 0, 0, tiled=True)
    return lax.dot_general(
        place, delta.reshape(slots, ho), (((0,), (0,)), ((), ())), preferred_element_type=F32
    ).astype(BF16)


def solution(mesh):
    groups, tp = mesh.shape["group"], mesh.shape["tp"]

    def on_device(tokens, w_query, adapter_down, adapter_up, adapter_id):
        gathered = lax.all_gather(tokens, "tp", axis=1, tiled=True)
        delta = lora(tokens, adapter_down, adapter_up, adapter_id, groups, tp)
        delta, gathered = lax.optimization_barrier((delta, gathered))
        base = lax.optimization_barrier(jnp.dot(gathered, w_query, preferred_element_type=F32))
        return (base + delta.astype(F32)).astype(BF16)

    placed = (
        P("group", "tp"),
        P(None, "tp"),
        P("group", None, "tp"),
        P("group", None, "tp"),
        P("group"),
    )
    return jax.shard_map(
        on_device, mesh=mesh, in_specs=placed, out_specs=P("group", "tp"), check_vma=False
    )
```
